32 devices in a mesh: group: 2 (over x), cell: 16 (over z, y, core).
Axes of the slice: x: 2, y: 2, z: 4, core: 2. Of those that a mesh axis runs over, the one named last changes fastest.
Arguments:
- scen_inputs: float32 [384, 4], P('cell'), may hold values from -1 to 1
- yields: bfloat16 [384, 10, 64, 256], P('cell', None, None, 'group'), parts along dimension 3, may hold values from -6 to 6
- crop_mask: int32 [64, 256], P('cell', 'group'), parts along dimension 1, may hold values 0 or 1
Outputs:
- coefs: float32 [64, 34, 256], P('cell', None, 'group'), parts along dimension 2
- residual: float32 [64, 34, 256], P('cell', None, 'group'), parts along dimension 2
The draws below stay inside these ranges and needn't reach their ends.
There are 2 independent parts, one for each index of `group`. The reference program is written for one: setup_inputs(seed, part) draws one part's arguments, and reference() takes and returns one part's arrays. A program takes and returns all parts, laid end to end along the dimension named above; an argument that names none is the same for every part. Nothing has to cross between parts.
All inputs are finite; a program needn't handle non-finite values. No bound on the sum of `crop_mask` on one device may be relied on, other than what follows from the above.
Results may differ from the reference program's by a relative error of at most 0.0026.
Values sent between devices are 32-bit elements; how exact they have to be, the bound alone decides.
A program may use at most 64 MiB of HBM per device.

```python
import jax
import jax.numpy as jnp
from jax import lax

YEARS = 10
ITERS = 3
TW = 128
SCEN = 384
NROWS = 64


def set_ends(drawn, key, least, largest):
    longest = drawn.shape.index(max(drawn.shape))
    spots = []
    for shift in (0, 1):
        where = [jax.random.randint(jax.random.fold_in(key, axis), (), 0, length) for axis, length in enumerate(drawn.shape)]
        where[longest] = (where[longest] + shift) % drawn.shape[longest]
        spots.append(tuple(where))
    return drawn.at[spots[0]].set(least).at[spots[1]].set(largest)


def raised(entries, own_key, source, target, blocks, factor):
    owner, partner = [(jnp.arange(entries.shape[axis_at]) // (entries.shape[axis_at] // blocks)).reshape([-1 if axis == axis_at else 1 for axis in range(entries.ndim)]) for axis_at in (source, target)]
    chosen = jax.random.permutation(own_key, blocks)[partner]
    strong = (owner == chosen) | (owner == (partner + blocks // 2) % blocks)
    return jnp.where(strong, factor * entries, entries)


def shard_levels(rng, dims, pieces, least, top_value):
    gain = 1.0
    for axis_at, blocks in pieces:
        draws = jax.random.uniform(jax.random.fold_in(jax.random.fold_in(rng, 6), axis_at), (blocks,), jnp.float32, least / len(pieces), top_value / len(pieces))
        gain = gain * jnp.repeat(jnp.exp(draws), dims[axis_at] // blocks).reshape((-1,) + (1,) * (len(dims) - 1 - axis_at))
    return gain


def bell_draw_with(stream_key, shape, deviation, reach, pieces, heavy, held_as=jnp.bfloat16):
    drawn = deviation * jax.random.normal(stream_key, shape, jnp.float32)
    if pieces:
        drawn = drawn * shard_levels(stream_key, shape, pieces, -0.22, 0.18)
    return jnp.clip(raised(drawn, jax.random.fold_in(stream_key, 3), *heavy), -reach, reach).astype(held_as)


def setup_inputs(seed: int = 0, part: int = 0) -> dict:
    key_of = jax.random.split(jax.random.key(seed), 4)
    own_keys = jax.random.split(jax.random.fold_in(key_of[3], part), 4)
    scen_inputs = jnp.clip(jax.random.uniform(key_of[0], (SCEN, 4), jnp.float32, -1.0, 1.0) * shard_levels(key_of[0], (SCEN, 4), ((0, 16),), -0.4, 0.0), -1.0, 1.0)
    yields = bell_draw_with(own_keys[1], (SCEN, YEARS, NROWS, TW), 1.0, 6.0, ((0, 16),), (0, 2, 16, 2.0))
    crop_mask = set_ends((jax.random.randint(own_keys[2], (NROWS, TW), 0, 4) < 3).astype(jnp.int32), jax.random.fold_in(own_keys[2], 1), 0, 1)
    return dict(scen_inputs=scen_inputs, yields=yields, crop_mask=crop_mask)


lambda_smooth = 0.5
ridge_term = 0.05


def design_terms(levels):
    parts = [levels[:, 0], levels[:, 1], levels[:, 2], levels[:, 3]]
    columns = [jnp.ones_like(parts[0])] + parts + [a * a for a in parts]
    for i in range(4):
        for j in range(i + 1, 4):
            columns.append(parts[i] * parts[j])
    columns = columns + [a * a * a for a in parts]
    for i in range(4):
        for j in range(4):
            if i != j:
                columns.append(parts[i] * parts[i] * parts[j])
    carbon, temper, water, nitro = parts
    columns = columns + [carbon * temper * water, carbon * temper * nitro, carbon * water * nitro]
    return jnp.stack(columns, axis=1)


def edge_weights(padded):
    center = padded[1:-1].astype(jnp.float32)
    north = padded[:-2].astype(jnp.float32)
    south = padded[2:].astype(jnp.float32)

    def link(near):
        return jnp.where(near >= 0.0, 0.25 + 0.75 * center * near, 0.0)

    east = jnp.roll(center, -1, axis=1)
    west = jnp.roll(center, 1, axis=1)
    stacked = [link(north), link(south), link(east), link(west), center]
    return [v[:, None, :] for v in stacked]


def apply_operator(field, padded_field, gram, weights):
    w_north, w_south, w_east, w_west, cropland = weights
    north = padded_field[:-2]
    south = padded_field[2:]
    lapl = w_north * (field - north) + w_south * (field - south)
    lapl = lapl + w_east * (field - jnp.roll(field, -1, axis=2)) + w_west * (field - jnp.roll(field, 1, axis=2))
    data = cropland * jnp.einsum("kj,rjw->rkw", gram, field, precision=lax.Precision.HIGHEST)
    return data + lambda_smooth * lapl + ridge_term * field


def reference(scen_inputs, yields, crop_mask):
    design = design_terms(scen_inputs)
    design_low = design.astype(jnp.bfloat16)
    gram = jnp.dot(design.T, design, precision=lax.Precision.HIGHEST) / SCEN
    summed = jnp.sum(yields.astype(jnp.float32), axis=1)
    rhs = jnp.einsum("sk,srw->rkw", design_low.astype(jnp.float32), summed, precision=lax.Precision.HIGHEST) / (SCEN * YEARS)
    padded_mask = jnp.pad(crop_mask, ((1, 1), (0, 0)), constant_values=-1)
    weights = edge_weights(padded_mask)
    coefs = jnp.zeros_like(rhs)
    residual = rhs
    direction = rhs
    norm_now = jnp.sum(residual * residual)
    for step in range(ITERS):
        padded_dir = jnp.pad(direction, ((1, 1), (0, 0), (0, 0)))
        image = apply_operator(direction, padded_dir, gram, weights)
        alpha = norm_now / jnp.sum(direction * image)
        coefs = coefs + alpha * direction
        residual = residual - alpha * image
        norm_next = jnp.sum(residual * residual)
        direction = residual + (norm_next / norm_now) * direction
        norm_now = norm_next
    return coefs, residual
```

```python
import functools

import jax
import jax.numpy as jnp
import numpy as np
from jax import lax
from jax.experimental import pallas as pl
from jax.experimental.pallas import tpu as pltpu
from jax.sharding import PartitionSpec as P

ITERS = 3
TERMS = 34
HALF = TERMS // 2
HROWS = HALF * 8
KROWS = TERMS * 8
PACKED = (HALF + 1) // 2
LAMBDA = 0.5
RIDGE = 0.05
MESH = pl.DeviceIdType.MESH
HIGHEST = lax.Precision.HIGHEST
F32 = jnp.float32
BF16 = jnp.bfloat16


def term_factors():
    terms = [(4, 4, 4)] + [(a, 4, 4) for a in range(4)] + [(a, a, 4) for a in range(4)]
    terms += [(i, j, 4) for i in range(4) for j in range(i + 1, 4)]
    terms += [(a, a, a) for a in range(4)]
    terms += [(i, i, j) for i in range(4) for j in range(4) if i != j]
    terms += [(0, 1, 2), (0, 1, 3), (0, 2, 3)]
    chosen = np.zeros((3, 40, 8), np.float32)
    for k, factors in enumerate(terms):
        for place, level in enumerate(factors):
            chosen[place, k, level] = 1.0
    return chosen.reshape(120, 8)


def iota(shape, dim):
    return lax.broadcasted_iota(jnp.int32, shape, dim)


def dot_nt(a, b, precision=None):
    return lax.dot_general(
        a, b, (((1,), (1,)), ((), ())), precision=precision, preferred_element_type=F32
    )


def dot_nn(a, b, precision=None):
    return jnp.dot(a, b, precision=precision, preferred_element_type=F32)


def three_parts(x):
    first = x.astype(BF16)
    rest = x - first.astype(F32)
    second = rest.astype(BF16)
    third = (rest - second.astype(F32)).astype(BF16)
    return first, second, third


def kernel(n, scen_ref, sel_ref, mask_ref, y_ref, coefs_ref, res_ref,
           ybuf, sbuf, part, r1, r2, r3, chip, pack_up, pack_low, halo, mwin, mhalo,
           lvl, mom, lhs_ref,
           ysem, s1s, s1r, s2s, s2r, s3s, s3r, cs, cr, hs, hr, ms, mr, ls, lr, ps, pr):
    nz = n // 4
    me = lax.axis_index("cell")
    core = me % 2
    mine_y = (me // 2) % 2
    mine_z = me // 4
    chip_id = me // 2
    chips = n // 2
    sibling = me + 1 - 2 * core
    across = me + 2 - 4 * mine_y
    scens, years = y_ref.shape[0], y_ref.shape[1]
    total = scens * n

    def zone(i):
        return (mine_z + 1 + i) % nz

    def load(i):
        rows = pl.ds(pl.multiple_of(zone(i) * 16, 16), 16)
        return pltpu.make_async_copy(y_ref.at[:, :, rows, :], ybuf.at[i], ysem.at[i])

    for i in range(nz):
        load(i).start()

    barrier = pltpu.get_barrier_semaphore()

    def greet(o, carry):
        pl.semaphore_signal(barrier, inc=1, device_id={"cell": (me + o) % n}, device_id_type=MESH)
        return carry

    lax.fori_loop(1, n, greet, 0)

    spots = (iota((8, 4), 0) == iota((8, 4), 1)).astype(F32)
    turned = dot_nt(spots, scen_ref[...], HIGHEST)
    own = jnp.concatenate([turned, jnp.zeros((8, 128 - scens), F32)], axis=1)
    own = own + ((iota((8, 128), 0) == 4) & (iota((8, 128), 1) < scens)).astype(F32)
    lvl[me] = own

    def copy(src, dst, send, recv, to):
        return pltpu.make_async_remote_copy(
            src_ref=src, dst_ref=dst, send_sem=send, recv_sem=recv,
            device_id={"cell": to}, device_id_type=MESH,
        )

    mask_down = copy(mask_ref, mhalo.at[0], ms.at[0], mr.at[0], (me + 1) % n)
    mask_up = copy(mask_ref, mhalo.at[1], ms.at[1], mr.at[1], (me + n - 1) % n)

    pl.semaphore_wait(barrier, n - 1)

    def spread(buf, send, recv):
        def go(o, carry):
            copy(buf.at[me], buf.at[me], send.at[o], recv.at[me], (me + o) % n).start()
            return carry

        lax.fori_loop(1, n, go, 0)

    def gather(buf, send, recv):
        def go(o, carry):
            source = (me + o) % n
            copy(buf.at[source], buf.at[source], send.at[o], recv.at[source], source).wait_recv()
            return carry

        lax.fori_loop(1, n, go, 0)

    def drain(buf, send, recv):
        def go(o, carry):
            copy(buf.at[me], buf.at[me], send.at[o], recv.at[me], (me + o) % n).wait_send()
            return carry

        lax.fori_loop(1, n, go, 0)

    spread(lvl, ls, lr)
    mask_down.start()
    mask_up.start()

    def design_of(levels):
        factors = dot_nn(sel_ref[...], levels, HIGHEST)
        return factors[0:40] * factors[40:80] * factors[80:120]

    widen = (iota((KROWS, 40), 0) // 8 == iota((KROWS, 40), 1)).astype(BF16)
    low = design_of(own).astype(BF16)
    tall = dot_nn(widen, low).astype(BF16)
    by_scen = (iota((scens * 8, 128), 0) // 8 == iota((scens * 8, 128), 1)).astype(BF16)
    full = dot_nt(tall, by_scen)
    same_row = iota((KROWS, scens * 8), 0) % 8 == iota((KROWS, scens * 8), 1) % 8
    lhs_ref[...] = jnp.where(same_row, full, 0.0).astype(BF16)

    def stage1(i):
        return copy(part.at[i, 1 - core], r1.at[i], s1s.at[i], s1r.at[i], sibling)

    def stage2(i):
        return copy(part.at[i, core, 1 - mine_y], r2.at[i], s2s.at[i], s2r.at[i], across)

    def stage3(i):
        to = zone(i) * 4 + me % 4
        return copy(part.at[i, core, mine_y], r3.at[mine_z], s3s.at[i], s3r.at[mine_z], to)

    def compute(i):
        load(i).wait()

        def years_of(s, carry):
            added = jnp.sum(ybuf[i, s].astype(F32), axis=0)
            rows = pl.ds(pl.multiple_of(s * 8, 8), 8)
            sbuf[rows, 0:128] = added[0:8]
            sbuf[rows, 128:256] = added[8:16]
            return carry

        lax.fori_loop(0, scens, years_of, 0, unroll=4)
        lhs = lhs_ref[...]
        first, second, third = three_parts(sbuf[...])
        prod = dot_nn(lhs, first) + (dot_nn(lhs, second) + dot_nn(lhs, third))
        for h in range(2):
            for y in range(2):
                part[i, h, y] = prod[h * HROWS:(h + 1) * HROWS, y * 128:(y + 1) * 128]
        stage1(i).start()

    def finish1(i):
        stage1(i).wait_recv()
        part[i, core, 1 - mine_y] = part[i, core, 1 - mine_y] + r1[i, 1 - mine_y]
        stage2(i).start()

    def finish2(i):
        stage2(i).wait_recv()
        added = part[i, core, mine_y] + r1[i, mine_y] + r2[i]
        if i < nz - 1:
            part[i, core, mine_y] = added
            stage3(i).start()
        else:
            r3[mine_z] = added

    for i in range(nz):
        compute(i)
        if i >= 1:
            finish1(i - 1)
        if i >= 2:
            finish2(i - 2)
    finish1(nz - 1)
    if nz >= 2:
        finish2(nz - 2)

    gather(lvl, ls, lr)
    levels = jnp.concatenate([lvl[i] for i in range(n)], axis=1)
    design = design_of(levels)
    gram = dot_nt(design, design, HIGHEST) * (1.0 / total)
    diag_block = iota((KROWS, KROWS), 0) % 8 == iota((KROWS, KROWS), 1) % 8
    gram_parts = []
    for piece in three_parts(gram):
        wide = dot_nt(dot_nn(widen, piece).astype(BF16), widen)
        gram_parts.append(jnp.where(diag_block, wide, 0.0).astype(BF16))
    g1, g2, g3 = gram_parts

    mask_down_in = copy(mhalo.at[0], mhalo.at[0], ms.at[0], mr.at[0], (me + n - 1) % n)
    mask_up_in = copy(mhalo.at[1], mhalo.at[1], ms.at[1], mr.at[1], (me + 1) % n)
    mask_down_in.wait_recv()
    mask_up_in.wait_recv()
    mwin[0:4, :] = jnp.where(me > 0, mhalo[0].astype(F32), -1.0)
    mwin[4:8, :] = mask_ref[...].astype(F32)
    mwin[8:12, :] = jnp.where(me < n - 1, mhalo[1].astype(F32), -1.0)
    mwin[12:16, :] = jnp.full((4, 128), -1.0, F32)
    center_a, center_b = mwin[0:8, :], mwin[8:16, :]
    sub = iota((8, 128), 0)

    def north_south(a, b):
        axis = a.ndim - 2
        here = sub if a.ndim == 2 else sub[None]
        down_a, down_b = pltpu.roll(a, 1, axis), pltpu.roll(b, 1, axis)
        up_a, up_b = pltpu.roll(a, 7, axis), pltpu.roll(b, 7, axis)
        return (down_a, jnp.where(here == 0, down_a, down_b),
                jnp.where(here == 7, up_b, up_a), up_b)

    def sides(a):
        axis = a.ndim - 1
        return pltpu.roll(a, 127, axis), pltpu.roll(a, 1, axis)

    north_a, north_b, south_a, south_b = north_south(center_a, center_b)

    def weights_of(center, north, south):
        def link(near):
            return jnp.where(near >= 0.0, 0.25 + 0.75 * center * near, 0.0) * LAMBDA

        east, west = sides(center)
        links = [link(north), link(south), link(east), link(west)]
        return links + [links[0] + links[1] + links[2] + links[3] + RIDGE, center]

    weights_a = weights_of(center_a, north_a, south_a)
    weights_b = weights_of(center_b, north_b, south_b)

    finish2(nz - 1)
    for j in range(1, nz):
        source = (mine_z + j) % nz
        copy(r3.at[source], r3.at[source], s3s.at[0], s3r.at[source], source * 4 + me % 4).wait_recv()
    summed = r3[0]
    for z in range(1, nz):
        summed = summed + r3[z]
    summed = summed * (1.0 / (total * years))
    chip[core] = summed
    swap = copy(chip.at[core], chip.at[core], cs, cr.at[core], sibling)
    swap.start()
    tiles = summed.reshape(HALF, 8, 128)
    front = tiles[0:PACKED]
    back = jnp.concatenate([tiles[PACKED:HALF], tiles[PACKED - 1:PACKED]], axis=0)
    upper = sub[None] < 4
    pack_up[...] = jnp.where(upper, pltpu.roll(front, 4, 1), back).reshape(PACKED * 8, 128)
    pack_low[...] = jnp.where(upper, front, pltpu.roll(back, 4, 1)).reshape(PACKED * 8, 128)
    send_up = copy(pack_up, halo.at[core], hs.at[0], hr.at[core], ((chip_id + 1) % chips) * 2)
    send_low = copy(pack_low, halo.at[core], hs.at[1], hr.at[core], ((chip_id + chips - 1) % chips) * 2 + 1)
    send_up.start()
    send_low.start()
    copy(chip.at[1 - core], chip.at[1 - core], cs, cr.at[1 - core], sibling).wait_recv()
    near_chip = jnp.where(core == 0, (chip_id + chips - 1) % chips, (chip_id + 1) % chips)
    for h in range(2):
        copy(halo.at[h], halo.at[h], hs.at[0], hr.at[h], near_chip * 2 + h).wait_recv()
    inside = jnp.where(core == 0, chip_id > 0, chip_id < chips - 1)
    edge = []
    for h in range(2):
        got = halo[h].reshape(PACKED, 8, 128)
        edge += [got, pltpu.roll(got[0:HALF - PACKED], 4, 1)]
    edge = jnp.concatenate(edge, axis=0)
    edge = jnp.where(inside, edge, 0.0)
    whole = jnp.concatenate([chip[0], chip[1]], axis=0).reshape(TERMS, 8, 128)
    moved = pltpu.roll(whole, 4, 1)
    first = core == 0
    v0a = jnp.where(first, jnp.where(upper, edge, moved), whole)
    v0b = jnp.where(first, moved, edge)

    def gram_times(field):
        f1, f2, f3 = three_parts(field)
        small = dot_nn(g3, f1) + dot_nn(g1, f3) + dot_nn(g2, f2)
        return dot_nn(g1, f1) + ((dot_nn(g2, f1) + dot_nn(g1, f2)) + small)

    def image_of(tile, north, south, data, weights):
        w_n, w_s, w_e, w_w, w_all, crop = [w[None] for w in weights]
        east, west = sides(tile)
        out = w_all * tile - w_n * north - w_s * south - w_e * east - w_w * west
        return out + crop * data

    def operator(a, b, both):
        n_a, n_b, s_a, s_b = north_south(a, b)
        flat = a.reshape(KROWS, 128)
        if both:
            flat = jnp.concatenate([flat, b.reshape(KROWS, 128)], axis=1)
        data = gram_times(flat)
        out_a = image_of(a, n_a, s_a, data[:, 0:128].reshape(TERMS, 8, 128), weights_a)
        if not both:
            return out_a, None
        return out_a, image_of(b, n_b, s_b, data[:, 128:256].reshape(TERMS, 8, 128), weights_b)

    v1a, v1b = operator(v0a, v0b, True)
    v2a, v2b = operator(v1a, v1b, True)
    v3a, _ = operator(v2a, v2b, False)

    pairs = [(v0a, v0a), (v0a, v1a), (v1a, v1a), (v1a, v2a), (v2a, v2a), (v2a, v3a), (v3a, v3a)]
    packed = jnp.zeros((8, 128), F32)
    for j, (p, q) in enumerate(pairs):
        tile = jnp.sum(p * q, axis=0)
        row = jnp.sum(jnp.where(sub >= 4, tile, 0.0), axis=0, keepdims=True)
        packed = jnp.where(sub == j, row, packed)
    mom[me] = packed
    spread(mom, ps, pr)
    gather(mom, ps, pr)
    sums = mom[0]
    for i in range(1, n):
        sums = sums + mom[i]
    sums = jnp.broadcast_to(jnp.sum(sums, axis=1, keepdims=True), (8, 128))
    m = [sums[j:j + 1, :] for j in range(7)]

    one = jnp.ones((1, 128), F32)
    res, direction, coef = [one], [one], []
    norm = m[0]

    def inner(p, q, shift):
        out = None
        for i, a in enumerate(p):
            for j, b in enumerate(q):
                term = a * b * m[i + j + shift]
                out = term if out is None else out + term
        return out

    def plus(p, q):
        size = max(len(p), len(q))
        out = []
        for i in range(size):
            if i < len(p) and i < len(q):
                out.append(p[i] + q[i])
            else:
                out.append(p[i] if i < len(p) else q[i])
        return out

    for step in range(ITERS):
        alpha = norm / inner(direction, direction, 1)
        coef = plus(coef, [alpha * d for d in direction])
        zero = jnp.zeros((1, 128), F32)
        res = plus(res, [zero] + [-alpha * d for d in direction])
        if step < ITERS - 1:
            fresh = inner(res, res, 0)
            beta = fresh / norm
            direction = plus(res, [beta * d for d in direction])
            norm = fresh

    basis = [v0a, v1a, v2a, v3a]

    def combine(factors):
        out = factors[0][None] * basis[0]
        for f, v in zip(factors[1:], basis[1:]):
            out = out + f[None] * v
        return jnp.swapaxes(out, 0, 1)[4:8]

    coefs_ref[...] = combine(coef)
    res_ref[...] = combine(res)

    drain(lvl, ls, lr)
    drain(mom, ps, pr)
    mask_down.wait_send()
    mask_up.wait_send()
    for i in range(nz):
        stage1(i).wait_send()
        stage2(i).wait_send()
        if i < nz - 1:
            stage3(i).wait_send()
    swap.wait_send()
    send_up.wait_send()
    send_low.wait_send()


def body(n, scen_inputs, yields, crop_mask):
    nz = n // 4
    scens, years = yields.shape[0], yields.shape[1]
    vmem = pl.BlockSpec(memory_space=pltpu.VMEM)
    dma = pltpu.SemaphoreType.DMA
    out = jax.ShapeDtypeStruct((4, TERMS, 128), F32)
    return pl.pallas_call(
        functools.partial(kernel, n),
        out_shape=(out, out),
        in_specs=[vmem, vmem, vmem, pl.BlockSpec(memory_space=pl.ANY)],
        out_specs=(vmem, vmem),
        scratch_shapes=[
            pltpu.VMEM((nz, scens, years, 16, 128), BF16),
            pltpu.VMEM((scens * 8, 256), F32),
            pltpu.VMEM((nz, 2, 2, HROWS, 128), F32),
            pltpu.VMEM((nz, 2, HROWS, 128), F32),
            pltpu.VMEM((nz, HROWS, 128), F32),
            pltpu.VMEM((nz, HROWS, 128), F32),
            pltpu.VMEM((2, HROWS, 128), F32),
            pltpu.VMEM((PACKED * 8, 128), F32),
            pltpu.VMEM((PACKED * 8, 128), F32),
            pltpu.VMEM((2, PACKED * 8, 128), F32),
            pltpu.VMEM((16, 128), F32),
            pltpu.VMEM((2, 4, 128), jnp.int32),
            pltpu.VMEM((n, 8, 128), F32),
            pltpu.VMEM((n, 8, 128), F32),
            pltpu.VMEM((KROWS, scens * 8), BF16),
            dma((nz,)),
            dma((nz,)), dma((nz,)),
            dma((nz,)), dma((nz,)),
            dma((nz,)), dma((nz,)),
            dma, dma((2,)),
            dma((2,)), dma((2,)),
            dma((2,)), dma((2,)),
            dma((n,)), dma((n,)),
            dma((n,)), dma((n,)),
        ],
        compiler_params=pltpu.CompilerParams(
            collective_id=0, has_side_effects=True, vmem_limit_bytes=48 * 1024 * 1024
        ),
    )(scen_inputs, jnp.asarray(term_factors()), crop_mask, yields)


def solution(mesh):
    in_specs = (P("cell", None), P("cell", None, None, "group"), P("cell", "group"))
    out_specs = (P("cell", None, "group"), P("cell", None, "group"))
    return jax.shard_map(
        functools.partial(body, mesh.shape["cell"]),
        mesh=mesh, in_specs=in_specs, out_specs=out_specs, check_vma=False,
    )
```

```python
import functools

import jax
import jax.numpy as jnp
import numpy as np
from jax import lax
from jax.experimental import pallas as pl
from jax.experimental.pallas import tpu as pltpu
from jax.sharding import PartitionSpec as P

TERMS = 34
HALF = TERMS // 2
HROWS = HALF * 8
KROWS = TERMS * 8
PACKED = (HALF + 1) // 2
LAMBDA = 0.5
RIDGE = 0.05
MESH = pl.DeviceIdType.MESH
HIGHEST = lax.Precision.HIGHEST
F32 = jnp.float32
BF16 = jnp.bfloat16


def term_factors():
    terms = [(4, 4, 4)] + [(a, 4, 4) for a in range(4)] + [(a, a, 4) for a in range(4)]
    terms += [(i, j, 4) for i in range(4) for j in range(i + 1, 4)]
    terms += [(a, a, a) for a in range(4)]
    terms += [(i, i, j) for i in range(4) for j in range(4) if i != j]
    terms += [(0, 1, 2), (0, 1, 3), (0, 2, 3)]
    chosen = np.zeros((3, 40, 8), np.float32)
    for k, factors in enumerate(terms):
        for place, level in enumerate(factors):
            chosen[place, k, level] = 1.0
    return chosen.reshape(120, 8)


def iota(shape, dim):
    return lax.broadcasted_iota(jnp.int32, shape, dim)


def dot_nt(a, b, precision=None):
    return lax.dot_general(
        a, b, (((1,), (1,)), ((), ())), precision=precision, preferred_element_type=F32
    )


def dot_nn(a, b, precision=None):
    return jnp.dot(a, b, precision=precision, preferred_element_type=F32)


def two_parts(x):
    first = x.astype(BF16)
    return first, (x - first.astype(F32)).astype(BF16)


def kernel(n, scen_hbm, sel_hbm, mask_hbm, y_ref, coefs_ref, res_ref,
           scen_ref, sel_ref, mask_ref,
           ybuf, sbuf, part, r1, r2, r3, chip, pack_up, pack_low, halo, mwin, mhalo,
           lvl, mom_a, mom_b, lhs_ref,
           ins, ysem, s1s, s1r, s2s, s2r, s3s, s3r, cs, cr, hs, hr, ms, mr, ls, lr, pas, par, pbs, pbr):
    nz = n // 4
    me = lax.axis_index("cell")
    core = me % 2
    mine_y = (me // 2) % 2
    mine_z = me // 4
    chip_id = me // 2
    chips = n // 2
    sibling = me + 1 - 2 * core
    across = me + 2 - 4 * mine_y
    scens, years = y_ref.shape[0], y_ref.shape[1]
    total = scens * n

    def zone(i):
        return (mine_z + 1 + i) % nz

    def load(i):
        rows = pl.ds(pl.multiple_of(zone(i) * 16, 16), 16)
        return pltpu.make_async_copy(y_ref.at[:, :, rows, :], ybuf.at[i], ysem.at[i])

    small = [
        pltpu.make_async_copy(scen_hbm, scen_ref, ins.at[0]),
        pltpu.make_async_copy(sel_hbm, sel_ref, ins.at[1]),
        pltpu.make_async_copy(mask_hbm, mask_ref, ins.at[2]),
    ]
    for move in small:
        move.start()
    for i in range(nz):
        load(i).start()

    barrier = pltpu.get_barrier_semaphore()

    def greet(o, carry):
        pl.semaphore_signal(barrier, inc=1, device_id={"cell": lax.rem(me + o, n)}, device_id_type=MESH)
        return carry

    lax.fori_loop(1, n, greet, 0)

    for move in small:
        move.wait()
    turned = jnp.concatenate([scen_ref[...], jnp.zeros((4, 128 - scens), F32)], axis=1)
    own = jnp.concatenate([turned, jnp.zeros((4, 128), F32)], axis=0)
    own = own + ((iota((8, 128), 0) == 4) & (iota((8, 128), 1) < scens)).astype(F32)
    lvl[me] = own

    def copy(src, dst, send, recv, to):
        return pltpu.make_async_remote_copy(
            src_ref=src, dst_ref=dst, send_sem=send, recv_sem=recv,
            device_id={"cell": to}, device_id_type=MESH,
        )

    mask_down = copy(mask_ref, mhalo.at[0], ms.at[0], mr.at[0], (me + 1) % n)
    mask_up = copy(mask_ref, mhalo.at[1], ms.at[1], mr.at[1], (me + n - 1) % n)

    def spread(buf, send, recv):
        for o in range(1, n):
            copy(buf.at[me], buf.at[me], send, recv, lax.rem(me + o, n)).start()

    def all_but_one(buf, send, recv):
        others = buf.at[pl.ds(0, n - 1)]
        return copy(others, others, send, recv, sibling)

    def design_of(levels):
        factors = dot_nn(sel_ref[...], levels, HIGHEST)
        return factors[0:40] * factors[40:80] * factors[80:120]

    widen = (iota((KROWS, 40), 0) // 8 == iota((KROWS, 40), 1)).astype(BF16)
    low = design_of(own).astype(BF16)
    tall = dot_nn(widen, low).astype(BF16)
    by_scen = (iota((scens * 8, 128), 0) // 8 == iota((scens * 8, 128), 1)).astype(BF16)
    full = dot_nt(tall, by_scen)
    same_row = iota((KROWS, scens * 8), 0) % 8 == iota((KROWS, scens * 8), 1) % 8
    lhs_ref[...] = jnp.where(same_row, full, 0.0).astype(BF16)

    def stage1(i):
        return copy(part.at[i, 1 - core], r1.at[i], s1s.at[i], s1r.at[i], sibling)

    def stage2(i):
        return copy(part.at[i, core, 1 - mine_y], r2.at[i], s2s.at[i], s2r.at[i], across)

    def stage3(i):
        to = zone(i) * 4 + me % 4
        return copy(part.at[i, core, mine_y], r3.at[mine_z], s3s.at[i], s3r.at[mine_z], to)

    def compute(i):
        load(i).wait()

        def years_of(s, carry):
            added = jnp.sum(ybuf[i, s].astype(F32), axis=0)
            rows = pl.ds(pl.multiple_of(s * 8, 8), 8)
            sbuf[rows, 0:128] = added[0:8]
            sbuf[rows, 128:256] = added[8:16]
            return carry

        lax.fori_loop(0, scens, years_of, 0, unroll=4)
        lhs = lhs_ref[...]
        first, second = two_parts(sbuf[...])
        prod = dot_nn(lhs, first) + dot_nn(lhs, second)
        for h in range(2):
            for y in range(2):
                part[i, h, y] = prod[h * HROWS:(h + 1) * HROWS, y * 128:(y + 1) * 128]
        if i == 0:
            pl.semaphore_wait(barrier, n - 1)
        stage1(i).start()
        if i == 0:
            spread(lvl, ls, lr)
            mask_down.start()
            mask_up.start()

    def finish1(i):
        stage1(i).wait_recv()
        part[i, core, 1 - mine_y] = part[i, core, 1 - mine_y] + r1[i, 1 - mine_y]
        stage2(i).start()

    def finish2(i):
        stage2(i).wait_recv()
        added = part[i, core, mine_y] + r1[i, mine_y] + r2[i]
        if i < nz - 1:
            part[i, core, mine_y] = added
            stage3(i).start()
        else:
            r3[mine_z] = added

    for i in range(nz):
        compute(i)
        if i >= 1:
            finish1(i - 1)
        if i >= 2:
            finish2(i - 2)
    finish1(nz - 1)
    if nz >= 2:
        finish2(nz - 2)

    all_but_one(lvl, ls, lr).wait_recv()
    levels = jnp.concatenate([lvl[i] for i in range(n)], axis=1)
    design = design_of(levels)
    gram = dot_nt(design, design, HIGHEST) * (1.0 / total)
    diag_block = iota((KROWS, KROWS), 0) % 8 == iota((KROWS, KROWS), 1) % 8
    gram_parts = []
    for piece in two_parts(gram):
        wide = dot_nt(dot_nn(widen, piece).astype(BF16), widen)
        gram_parts.append(jnp.where(diag_block, wide, 0.0).astype(BF16))
    g1, g2 = gram_parts

    mask_down_in = copy(mhalo.at[0], mhalo.at[0], ms.at[0], mr.at[0], (me + n - 1) % n)
    mask_up_in = copy(mhalo.at[1], mhalo.at[1], ms.at[1], mr.at[1], (me + 1) % n)
    mask_down_in.wait_recv()
    mask_up_in.wait_recv()
    mwin[0:4, :] = jnp.where(me > 0, mhalo[0].astype(F32), -1.0)
    mwin[4:8, :] = mask_ref[...].astype(F32)
    mwin[8:12, :] = jnp.where(me < n - 1, mhalo[1].astype(F32), -1.0)
    mwin[12:16, :] = jnp.full((4, 128), -1.0, F32)
    center_a, center_b = mwin[0:8, :], mwin[8:16, :]
    sub = iota((8, 128), 0)

    def north_south(a, b):
        axis = a.ndim - 2
        here = sub if a.ndim == 2 else sub[None]
        down_a, down_b = pltpu.roll(a, 1, axis), pltpu.roll(b, 1, axis)
        up_a, up_b = pltpu.roll(a, 7, axis), pltpu.roll(b, 7, axis)
        return (down_a, jnp.where(here == 0, down_a, down_b),
                jnp.where(here == 7, up_b, up_a), up_b)

    def sides(a):
        axis = a.ndim - 1
        return pltpu.roll(a, 127, axis), pltpu.roll(a, 1, axis)

    north_a, north_b, south_a, south_b = north_south(center_a, center_b)

    def weights_of(center, north, south):
        def link(near):
            return jnp.where(near >= 0.0, 0.25 + 0.75 * center * near, 0.0) * LAMBDA

        east, west = sides(center)
        links = [link(north), link(south), link(east), link(west)]
        return links + [links[0] + links[1] + links[2] + links[3] + RIDGE, center]

    weights_a = weights_of(center_a, north_a, south_a)
    weights_b = weights_of(center_b, north_b, south_b)

    finish2(nz - 1)
    for j in range(1, nz):
        source = (mine_z + j) % nz
        copy(r3.at[source], r3.at[source], s3s.at[0], s3r.at[source], source * 4 + me % 4).wait_recv()
    summed = r3[0]
    for z in range(1, nz):
        summed = summed + r3[z]
    summed = summed * (1.0 / (total * years))
    chip[core] = summed
    swap = copy(chip.at[core], chip.at[core], cs, cr.at[core], sibling)
    swap.start()
    tiles = summed.reshape(HALF, 8, 128)
    front = tiles[0:PACKED]
    back = jnp.concatenate([tiles[PACKED:HALF], tiles[PACKED - 1:PACKED]], axis=0)
    upper = sub[None] < 4
    pack_up[...] = jnp.where(upper, pltpu.roll(front, 4, 1), back).reshape(PACKED * 8, 128)
    pack_low[...] = jnp.where(upper, front, pltpu.roll(back, 4, 1)).reshape(PACKED * 8, 128)
    send_up = copy(pack_up, halo.at[core], hs.at[0], hr.at[core], ((chip_id + 1) % chips) * 2)
    send_low = copy(pack_low, halo.at[core], hs.at[1], hr.at[core], ((chip_id + chips - 1) % chips) * 2 + 1)
    send_up.start()
    send_low.start()
    copy(chip.at[1 - core], chip.at[1 - core], cs, cr.at[1 - core], sibling).wait_recv()
    near_chip = jnp.where(core == 0, (chip_id + chips - 1) % chips, (chip_id + 1) % chips)
    for h in range(2):
        copy(halo.at[h], halo.at[h], hs.at[0], hr.at[h], near_chip * 2 + h).wait_recv()
    inside = jnp.where(core == 0, chip_id > 0, chip_id < chips - 1)
    edge = []
    for h in range(2):
        got = halo[h].reshape(PACKED, 8, 128)
        edge += [got, pltpu.roll(got[0:HALF - PACKED], 4, 1)]
    edge = jnp.concatenate(edge, axis=0)
    edge = jnp.where(inside, edge, 0.0)
    whole = jnp.concatenate([chip[0], chip[1]], axis=0).reshape(TERMS, 8, 128)
    moved = pltpu.roll(whole, 4, 1)
    first = core == 0
    v0a = jnp.where(first, jnp.where(upper, edge, moved), whole)
    v0b = jnp.where(first, moved, edge)

    def gram_times(field):
        f1, f2 = two_parts(field)
        return dot_nn(g1, f1) + (dot_nn(g2, f1) + dot_nn(g1, f2))

    def image_of(tile, north, south, data, weights):
        w_n, w_s, w_e, w_w, w_all, crop = [w[None] for w in weights]
        east, west = sides(tile)
        out = w_all * tile - w_n * north - w_s * south - w_e * east - w_w * west
        return out + crop * data

    def operator(a, b, both):
        n_a, n_b, s_a, s_b = north_south(a, b)
        flat = a.reshape(KROWS, 128)
        if both:
            flat = jnp.concatenate([flat, b.reshape(KROWS, 128)], axis=1)
        data = gram_times(flat)
        out_a = image_of(a, n_a, s_a, data[:, 0:128].reshape(TERMS, 8, 128), weights_a)
        if not both:
            return out_a, None
        return out_a, image_of(b, n_b, s_b, data[:, 128:256].reshape(TERMS, 8, 128), weights_b)

    def pack(pairs):
        packed = jnp.zeros((8, 128), F32)
        for j, (p, q) in enumerate(pairs):
            tile = jnp.sum(p * q, axis=0)
            row = jnp.sum(jnp.where(sub >= 4, tile, 0.0), axis=0, keepdims=True)
            packed = jnp.where(sub == j, row, packed)
        return packed

    def sums_of(buf):
        sums = buf[0]
        for i in range(1, n):
            sums = sums + buf[i]
        sums = jnp.broadcast_to(jnp.sum(sums, axis=1, keepdims=True), (8, 128))
        return [sums[j:j + 1, :] for j in range(7)]

    v1a, v1b = operator(v0a, v0b, True)
    mom_a[me] = pack([(v0a, v0a), (v0a, v1a), (v1a, v1a)])
    spread(mom_a, pas, par)
    v2a, v2b = operator(v1a, v1b, True)
    all_but_one(mom_a, pas, par).wait_recv()
    m = sums_of(mom_a)
    alpha0 = m[0] / m[1]
    beta0 = (m[0] - 2.0 * alpha0 * m[1] + alpha0 * alpha0 * m[2]) / m[0]
    res1 = v0a - alpha0 * v1a
    dir1 = res1 + beta0 * v0a
    image_res1 = v1a - alpha0 * v2a
    image1a = image_res1 + beta0 * v1a
    image1b = (v1b - alpha0 * v2b) + beta0 * v1b
    twice, _ = operator(image1a, image1b, False)

    mom_b[me] = pack([(res1, res1), (dir1, image1a), (res1, image1a), (image1a, image1a),
                      (res1, image_res1), (image1a, image_res1), (image1a, twice)])
    spread(mom_b, pbs, pbr)
    all_but_one(mom_b, pbs, pbr).wait_recv()
    rr, da, ra, aa, rt, at, aw = sums_of(mom_b)
    alpha1 = rr / da
    fresh = rr - 2.0 * alpha1 * ra + alpha1 * alpha1 * aa
    beta1 = fresh / rr
    along = (rt + 2.0 * beta1 * ra - 2.0 * alpha1 * at - 2.0 * alpha1 * beta1 * aa
             + alpha1 * alpha1 * aw + beta1 * beta1 * da)
    alpha2 = fresh / along
    res2 = res1 - alpha1 * image1a
    dir2 = res2 + beta1 * dir1
    image2 = image_res1 - alpha1 * twice + beta1 * image1a
    coefs_ref[...] = (alpha0 * v0a + alpha1 * dir1 + alpha2 * dir2)[:, 4:8, :]
    res_ref[...] = (res2 - alpha2 * image2)[:, 4:8, :]

    all_but_one(lvl, ls, lr).wait_send()
    all_but_one(mom_a, pas, par).wait_send()
    all_but_one(mom_b, pbs, pbr).wait_send()
    mask_down.wait_send()
    mask_up.wait_send()
    for i in range(nz):
        stage1(i).wait_send()
        stage2(i).wait_send()
        if i < nz - 1:
            stage3(i).wait_send()
    swap.wait_send()
    send_up.wait_send()
    send_low.wait_send()


def body(n, scen_inputs, yields, crop_mask):
    nz = n // 4
    scens, years = yields.shape[0], yields.shape[1]
    vmem = pl.BlockSpec(memory_space=pltpu.VMEM)
    hbm = pl.BlockSpec(memory_space=pltpu.HBM)
    dma = pltpu.SemaphoreType.DMA
    out = jax.ShapeDtypeStruct((TERMS, 4, 128), F32)
    coefs, residual = pl.pallas_call(
        functools.partial(kernel, n),
        out_shape=(out, out),
        in_specs=[hbm, hbm, hbm, hbm],
        out_specs=(vmem, vmem),
        scratch_shapes=[
            pltpu.VMEM((4, scens), F32),
            pltpu.VMEM((120, 8), F32),
            pltpu.VMEM((4, 128), jnp.int32),
            pltpu.VMEM((nz, scens, years, 16, 128), BF16),
            pltpu.VMEM((scens * 8, 256), F32),
            pltpu.VMEM((nz, 2, 2, HROWS, 128), F32),
            pltpu.VMEM((nz, 2, HROWS, 128), F32),
            pltpu.VMEM((nz, HROWS, 128), F32),
            pltpu.VMEM((nz, HROWS, 128), F32),
            pltpu.VMEM((2, HROWS, 128), F32),
            pltpu.VMEM((PACKED * 8, 128), F32),
            pltpu.VMEM((PACKED * 8, 128), F32),
            pltpu.VMEM((2, PACKED * 8, 128), F32),
            pltpu.VMEM((16, 128), F32),
            pltpu.VMEM((2, 4, 128), jnp.int32),
            pltpu.VMEM((n, 8, 128), F32),
            pltpu.VMEM((n, 8, 128), F32),
            pltpu.VMEM((n, 8, 128), F32),
            pltpu.VMEM((KROWS, scens * 8), BF16),
            dma((3,)), dma((nz,)),
            dma((nz,)), dma((nz,)),
            dma((nz,)), dma((nz,)),
            dma((nz,)), dma((nz,)),
            dma, dma((2,)),
            dma((2,)), dma((2,)),
            dma((2,)), dma((2,)),
            dma, dma, dma, dma, dma, dma,
        ],
        compiler_params=pltpu.CompilerParams(
            collective_id=0, has_side_effects=True, vmem_limit_bytes=64512 * 1024
        ),
    )(scen_inputs.T, jnp.asarray(term_factors()), crop_mask, yields)
    return jnp.transpose(coefs, (1, 0, 2)), jnp.transpose(residual, (1, 0, 2))


def solution(mesh):
    in_specs = (P("cell", None), P("cell", None, None, "group"), P("cell", "group"))
    out_specs = (P("cell", None, "group"), P("cell", None, "group"))
    return jax.shard_map(
        functools.partial(body, mesh.shape["cell"]),
        mesh=mesh, in_specs=in_specs, out_specs=out_specs, check_vma=False,
    )
```

```python
import functools

import jax
import jax.numpy as jnp
import numpy as np
from jax import lax
from jax.experimental import pallas as pl
from jax.experimental.pallas import tpu as pltpu
from jax.sharding import PartitionSpec as P

TERMS = 34
HALF = TERMS // 2
HROWS = HALF * 8
KROWS = TERMS * 8
PACKED = (HALF + 1) // 2
LAMBDA = 0.5
RIDGE = 0.05
MESH = pl.DeviceIdType.MESH
HIGHEST = lax.Precision.HIGHEST
F32 = jnp.float32
BF16 = jnp.bfloat16


def term_factors():
    terms = [(4, 4, 4)] + [(a, 4, 4) for a in range(4)] + [(a, a, 4) for a in range(4)]
    terms += [(i, j, 4) for i in range(4) for j in range(i + 1, 4)]
    terms += [(a, a, a) for a in range(4)]
    terms += [(i, i, j) for i in range(4) for j in range(4) if i != j]
    terms += [(0, 1, 2), (0, 1, 3), (0, 2, 3)]
    chosen = np.zeros((3, 40, 8), np.float32)
    for k, factors in enumerate(terms):
        for place, level in enumerate(factors):
            chosen[place, k, level] = 1.0
    return chosen.reshape(120, 8)


def iota(shape, dim):
    return lax.broadcasted_iota(jnp.int32, shape, dim)


def dot_nt(a, b, precision=None):
    return lax.dot_general(
        a, b, (((1,), (1,)), ((), ())), precision=precision, preferred_element_type=F32
    )


def dot_nn(a, b, precision=None):
    return jnp.dot(a, b, precision=precision, preferred_element_type=F32)


def two_parts(x):
    first = x.astype(BF16)
    return first, (x - first.astype(F32)).astype(BF16)


def kernel(n, scen_hbm, sel_hbm, mask_hbm, y_ref, out_ref,
           scen_ref, sel_ref, mask_ref,
           ybuf, sbuf, part, r1, r2, r3, chip, pack_up, pack_low, halo, mwin, mhalo,
           lvl, mom_a, mom_b, lhs_ref,
           ins, ysem, s1s, s1r, s2s, s2r, s3s, s3r, cs, cr, hs, hr, ms, mr, ls, lr, pas, par, pbs, pbr):
    nz = n // 4
    me = lax.axis_index("cell")
    core = me % 2
    mine_y = (me // 2) % 2
    mine_z = me // 4
    chip_id = me // 2
    chips = n // 2
    sibling = me + 1 - 2 * core
    across = me + 2 - 4 * mine_y
    scens, years = y_ref.shape[0], y_ref.shape[1]
    total = scens * n

    def zone(i):
        return (mine_z + 1 + i) % nz

    def load(i):
        rows = pl.ds(pl.multiple_of(zone(i) * 16, 16), 16)
        return pltpu.make_async_copy(y_ref.at[:, :, rows, :], ybuf.at[i], ysem.at[i])

    small = [
        pltpu.make_async_copy(scen_hbm, scen_ref, ins.at[0]),
        pltpu.make_async_copy(sel_hbm, sel_ref, ins.at[1]),
        pltpu.make_async_copy(mask_hbm, mask_ref, ins.at[2]),
    ]
    for move in small:
        move.start()
    for i in range(nz):
        load(i).start()

    barrier = pltpu.get_barrier_semaphore()

    def greet(o, carry):
        pl.semaphore_signal(barrier, inc=1, device_id={"cell": lax.rem(me + o, n)}, device_id_type=MESH)
        return carry

    lax.fori_loop(1, n, greet, 0)

    for move in small:
        move.wait()
    turned = jnp.concatenate([scen_ref[...], jnp.zeros((4, 128 - scens), F32)], axis=1)
    lvl[me] = turned
    filled = ((iota((4, 128), 0) == 0) & (iota((4, 128), 1) < scens)).astype(F32)
    own = jnp.concatenate([turned, filled], axis=0)

    def copy(src, dst, send, recv, to):
        return pltpu.make_async_remote_copy(
            src_ref=src, dst_ref=dst, send_sem=send, recv_sem=recv,
            device_id={"cell": to}, device_id_type=MESH,
        )

    mask_down = copy(mask_ref, mhalo.at[0], ms.at[0], mr.at[0], (me + 1) % n)
    mask_up = copy(mask_ref, mhalo.at[1], ms.at[1], mr.at[1], (me + n - 1) % n)

    def spread(buf, send, recv):
        for o in range(1, n):
            copy(buf.at[me], buf.at[me], send, recv, lax.rem(me + o, n)).start()

    def all_but_one(buf, send, recv):
        others = buf.at[pl.ds(0, n - 1)]
        return copy(others, others, send, recv, sibling)

    def design_of(levels):
        factors = dot_nn(sel_ref[...], levels, HIGHEST)
        return factors[0:40] * factors[40:80] * factors[80:120]

    widen = (iota((KROWS, 40), 0) // 8 == iota((KROWS, 40), 1)).astype(BF16)
    low = design_of(own).astype(BF16)
    tall = dot_nn(widen, low).astype(BF16)
    by_scen = (iota((scens * 8, 128), 0) // 8 == iota((scens * 8, 128), 1)).astype(BF16)
    full = dot_nt(tall, by_scen)
    same_row = iota((KROWS, scens * 8), 0) % 8 == iota((KROWS, scens * 8), 1) % 8
    lhs_ref[...] = jnp.where(same_row, full, 0.0).astype(BF16)

    def stage1(i):
        return copy(part.at[i, 1 - core], r1.at[i], s1s.at[i], s1r.at[i], sibling)

    def stage2(i):
        return copy(part.at[i, core, 1 - mine_y], r2.at[i], s2s.at[i], s2r.at[i], across)

    def stage3(i):
        to = zone(i) * 4 + me % 4
        return copy(part.at[i, core, mine_y], r3.at[mine_z], s3s.at[i], s3r.at[mine_z], to)

    def compute(i):
        load(i).wait()

        def years_of(s, carry):
            added = jnp.sum(ybuf[i, s].astype(F32), axis=0)
            rows = pl.ds(pl.multiple_of(s * 8, 8), 8)
            sbuf[rows, 0:128] = added[0:8]
            sbuf[rows, 128:256] = added[8:16]
            return carry

        lax.fori_loop(0, scens, years_of, 0, unroll=4)
        lhs = lhs_ref[...]
        first, second = two_parts(sbuf[...])
        prod = dot_nn(lhs, first) + dot_nn(lhs, second)
        for h in range(2):
            for y in range(2):
                part[i, h, y] = prod[h * HROWS:(h + 1) * HROWS, y * 128:(y + 1) * 128]
        if i == 0:
            pl.semaphore_wait(barrier, n - 1)
        stage1(i).start()
        if i == 0:
            spread(lvl, ls, lr)
            mask_down.start()
            mask_up.start()

    def finish1(i):
        stage1(i).wait_recv()
        part[i, core, 1 - mine_y] = part[i, core, 1 - mine_y] + r1[i, 1 - mine_y]
        stage2(i).start()

    def finish2(i):
        stage2(i).wait_recv()
        added = part[i, core, mine_y] + r1[i, mine_y] + r2[i]
        if i < nz - 1:
            part[i, core, mine_y] = added
            stage3(i).start()
        else:
            r3[mine_z] = added

    for i in range(nz):
        compute(i)
        if i >= 1:
            finish1(i - 1)
        if i >= 2:
            finish2(i - 2)
    finish1(nz - 1)
    if nz >= 2:
        finish2(nz - 2)

    all_but_one(lvl, ls, lr).wait_recv()
    levels = jnp.concatenate([lvl[i] for i in range(n)], axis=1)
    levels = jnp.concatenate([levels, jnp.concatenate([filled] * n, axis=1)], axis=0)
    design = design_of(levels)
    gram = dot_nt(design, design, HIGHEST) * (1.0 / total)
    diag_block = iota((KROWS, KROWS), 0) % 8 == iota((KROWS, KROWS), 1) % 8
    gram_parts = []
    for piece in two_parts(gram):
        wide = dot_nt(dot_nn(widen, piece).astype(BF16), widen)
        gram_parts.append(jnp.where(diag_block, wide, 0.0).astype(BF16))
    g1, g2 = gram_parts

    mask_down_in = copy(mhalo.at[0], mhalo.at[0], ms.at[0], mr.at[0], (me + n - 1) % n)
    mask_up_in = copy(mhalo.at[1], mhalo.at[1], ms.at[1], mr.at[1], (me + 1) % n)
    mask_down_in.wait_recv()
    mask_up_in.wait_recv()
    mwin[0:4, :] = jnp.where(me > 0, mhalo[0].astype(F32), -1.0)
    mwin[4:8, :] = mask_ref[...].astype(F32)
    mwin[8:12, :] = jnp.where(me < n - 1, mhalo[1].astype(F32), -1.0)
    mwin[12:16, :] = jnp.full((4, 128), -1.0, F32)
    center_a, center_b = mwin[0:8, :], mwin[8:16, :]
    sub = iota((8, 128), 0)

    def north_south(a, b):
        axis = a.ndim - 2
        here = sub if a.ndim == 2 else sub[None]
        down_a, down_b = pltpu.roll(a, 1, axis), pltpu.roll(b, 1, axis)
        up_a, up_b = pltpu.roll(a, 7, axis), pltpu.roll(b, 7, axis)
        return (down_a, jnp.where(here == 0, down_a, down_b),
                jnp.where(here == 7, up_b, up_a), up_b)

    def sides(a):
        axis = a.ndim - 1
        return pltpu.roll(a, 127, axis), pltpu.roll(a, 1, axis)

    north_a, north_b, south_a, south_b = north_south(center_a, center_b)

    def weights_of(center, north, south):
        def link(near):
            return jnp.where(near >= 0.0, 0.25 + 0.75 * center * near, 0.0) * LAMBDA

        east, west = sides(center)
        links = [link(north), link(south), link(east), link(west)]
        return links + [links[0] + links[1] + links[2] + links[3] + RIDGE, center]

    weights_a = weights_of(center_a, north_a, south_a)
    weights_b = weights_of(center_b, north_b, south_b)

    finish2(nz - 1)
    for j in range(1, nz):
        source = (mine_z + j) % nz
        copy(r3.at[source], r3.at[source], s3s.at[0], s3r.at[source], source * 4 + me % 4).wait_recv()
    summed = r3[0]
    for z in range(1, nz):
        summed = summed + r3[z]
    summed = summed * (1.0 / (total * years))
    chip[core] = summed
    swap = copy(chip.at[core], chip.at[core], cs, cr.at[core], sibling)
    swap.start()
    tiles = summed.reshape(HALF, 8, 128)
    front = tiles[0:PACKED]
    back = jnp.concatenate([tiles[PACKED:HALF], tiles[PACKED - 1:PACKED]], axis=0)
    upper = sub[None] < 4
    pack_up[...] = jnp.where(upper, pltpu.roll(front, 4, 1), back).reshape(PACKED * 8, 128)
    pack_low[...] = jnp.where(upper, front, pltpu.roll(back, 4, 1)).reshape(PACKED * 8, 128)
    send_up = copy(pack_up, halo.at[core], hs.at[0], hr.at[core], ((chip_id + 1) % chips) * 2)
    send_low = copy(pack_low, halo.at[core], hs.at[1], hr.at[core], ((chip_id + chips - 1) % chips) * 2 + 1)
    send_up.start()
    send_low.start()
    copy(chip.at[1 - core], chip.at[1 - core], cs, cr.at[1 - core], sibling).wait_recv()
    near_chip = jnp.where(core == 0, (chip_id + chips - 1) % chips, (chip_id + 1) % chips)
    for h in range(2):
        copy(halo.at[h], halo.at[h], hs.at[0], hr.at[h], near_chip * 2 + h).wait_recv()
    inside = jnp.where(core == 0, chip_id > 0, chip_id < chips - 1)
    edge = []
    for h in range(2):
        got = halo[h].reshape(PACKED, 8, 128)
        edge += [got, pltpu.roll(got[0:HALF - PACKED], 4, 1)]
    edge = jnp.concatenate(edge, axis=0)
    edge = jnp.where(inside, edge, 0.0)
    whole = jnp.concatenate([chip[0], chip[1]], axis=0).reshape(TERMS, 8, 128)
    moved = pltpu.roll(whole, 4, 1)
    first = core == 0
    v0a = jnp.where(first, jnp.where(upper, edge, moved), whole)
    v0b = jnp.where(first, moved, edge)

    def gram_times(field):
        f1, f2 = two_parts(field)
        return dot_nn(g1, f1) + (dot_nn(g2, f1) + dot_nn(g1, f2))

    def image_of(tile, north, south, data, weights):
        w_n, w_s, w_e, w_w, w_all, crop = [w[None] for w in weights]
        east, west = sides(tile)
        out = w_all * tile - w_n * north - w_s * south - w_e * east - w_w * west
        return out + crop * data

    def operator(a, b, both):
        n_a, n_b, s_a, s_b = north_south(a, b)
        flat = a.reshape(KROWS, 128)
        if both:
            flat = jnp.concatenate([flat, b.reshape(KROWS, 128)], axis=1)
        data = gram_times(flat)
        out_a = image_of(a, n_a, s_a, data[:, 0:128].reshape(TERMS, 8, 128), weights_a)
        if not both:
            return out_a, None
        return out_a, image_of(b, n_b, s_b, data[:, 128:256].reshape(TERMS, 8, 128), weights_b)

    def pack(pairs):
        packed = jnp.zeros((8, 128), F32)
        for j, (p, q) in enumerate(pairs):
            tile = jnp.sum(p * q, axis=0)
            row = jnp.sum(jnp.where(sub >= 4, tile, 0.0), axis=0, keepdims=True)
            packed = jnp.where(sub == j, row, packed)
        packed = jnp.sum(packed, axis=1, keepdims=True)
        return jnp.sum(jnp.where(sub == iota((8, 128), 1), packed, 0.0), axis=0, keepdims=True)

    def sums_of(buf):
        sums = buf[0]
        for i in range(1, n):
            sums = sums + buf[i]
        sums = jnp.where(sub == iota((8, 128), 1), sums, 0.0)
        sums = jnp.broadcast_to(jnp.sum(sums, axis=1, keepdims=True), (8, 128))
        return [sums[j:j + 1, :] for j in range(7)]

    v1a, v1b = operator(v0a, v0b, True)
    mom_a[me] = pack([(v0a, v0a), (v0a, v1a), (v1a, v1a)])
    spread(mom_a, pas, par)
    v2a, v2b = operator(v1a, v1b, True)
    all_but_one(mom_a, pas, par).wait_recv()
    m = sums_of(mom_a)
    alpha0 = m[0] / m[1]
    beta0 = (m[0] - 2.0 * alpha0 * m[1] + alpha0 * alpha0 * m[2]) / m[0]
    res1 = v0a - alpha0 * v1a
    dir1 = res1 + beta0 * v0a
    image_res1 = v1a - alpha0 * v2a
    image1a = image_res1 + beta0 * v1a
    image1b = (v1b - alpha0 * v2b) + beta0 * v1b
    twice, _ = operator(image1a, image1b, False)

    mom_b[me] = pack([(res1, res1), (dir1, image1a), (res1, image1a), (image1a, image1a),
                      (res1, image_res1), (image1a, image_res1), (image1a, twice)])
    spread(mom_b, pbs, pbr)
    all_but_one(mom_b, pbs, pbr).wait_recv()
    rr, da, ra, aa, rt, at, aw = sums_of(mom_b)
    alpha1 = rr / da
    fresh = rr - 2.0 * alpha1 * ra + alpha1 * alpha1 * aa
    beta1 = fresh / rr
    along = (rt + 2.0 * beta1 * ra - 2.0 * alpha1 * at - 2.0 * alpha1 * beta1 * aa
             + alpha1 * alpha1 * aw + beta1 * beta1 * da)
    alpha2 = fresh / along
    res2 = res1 - alpha1 * image1a
    dir2 = res2 + beta1 * dir1
    image2 = image_res1 - alpha1 * twice + beta1 * image1a
    solved = alpha0 * v0a + alpha1 * dir1 + alpha2 * dir2
    out_ref[...] = jnp.where(upper, pltpu.roll(solved, 4, 1), res2 - alpha2 * image2)

    all_but_one(lvl, ls, lr).wait_send()
    all_but_one(mom_a, pas, par).wait_send()
    all_but_one(mom_b, pbs, pbr).wait_send()
    mask_down.wait_send()
    mask_up.wait_send()
    for i in range(nz):
        stage1(i).wait_send()
        stage2(i).wait_send()
        if i < nz - 1:
            stage3(i).wait_send()
    swap.wait_send()
    send_up.wait_send()
    send_low.wait_send()


def body(n, scen_inputs, yields, crop_mask):
    nz = n // 4
    scens, years = yields.shape[0], yields.shape[1]
    vmem = pl.BlockSpec(memory_space=pltpu.VMEM)
    hbm = pl.BlockSpec(memory_space=pltpu.HBM)
    dma = pltpu.SemaphoreType.DMA
    both = pl.pallas_call(
        functools.partial(kernel, n),
        out_shape=jax.ShapeDtypeStruct((TERMS, 8, 128), F32),
        in_specs=[hbm, hbm, hbm, hbm],
        out_specs=vmem,
        scratch_shapes=[
            pltpu.VMEM((4, scens), F32),
            pltpu.VMEM((120, 8), F32),
            pltpu.VMEM((4, 128), jnp.int32),
            pltpu.VMEM((nz, scens, years, 16, 128), BF16),
            pltpu.VMEM((scens * 8, 256), F32),
            pltpu.VMEM((nz, 2, 2, HROWS, 128), F32),
            pltpu.VMEM((nz, 2, HROWS, 128), F32),
            pltpu.VMEM((nz, HROWS, 128), F32),
            pltpu.VMEM((nz, HROWS, 128), F32),
            pltpu.VMEM((2, HROWS, 128), F32),
            pltpu.VMEM((PACKED * 8, 128), F32),
            pltpu.VMEM((PACKED * 8, 128), F32),
            pltpu.VMEM((2, PACKED * 8, 128), F32),
            pltpu.VMEM((16, 128), F32),
            pltpu.VMEM((2, 4, 128), jnp.int32),
            pltpu.VMEM((n, 4, 128), F32),
            pltpu.VMEM((n, 1, 128), F32),
            pltpu.VMEM((n, 1, 128), F32),
            pltpu.VMEM((KROWS, scens * 8), BF16),
            dma((3,)), dma((nz,)),
            dma((nz,)), dma((nz,)),
            dma((nz,)), dma((nz,)),
            dma((nz,)), dma((nz,)),
            dma, dma((2,)),
            dma((2,)), dma((2,)),
            dma((2,)), dma((2,)),
            dma, dma, dma, dma, dma, dma,
        ],
        compiler_params=pltpu.CompilerParams(
            collective_id=0, has_side_effects=True, vmem_limit_bytes=64512 * 1024
        ),
    )(scen_inputs.T, jnp.asarray(term_factors()), crop_mask, yields)
    both = jnp.transpose(both, (1, 0, 2))
    return both[0:4], both[4:8]


def solution(mesh):
    in_specs = (P("cell", None), P("cell", None, None, "group"), P("cell", "group"))
    out_specs = (P("cell", None, "group"), P("cell", None, "group"))
    return jax.shard_map(
        functools.partial(body, mesh.shape["cell"]),
        mesh=mesh, in_specs=in_specs, out_specs=out_specs, check_vma=False,
    )
```

```python
import functools

import jax
import jax.numpy as jnp
import numpy as np
from jax import lax
from jax.experimental import pallas as pl
from jax.experimental.pallas import tpu as pltpu
from jax.sharding import PartitionSpec as P

TERMS = 34
HALF = TERMS // 2
HROWS = HALF * 8
KROWS = TERMS * 8
PACKED = (HALF + 1) // 2
LAMBDA = 0.5
RIDGE = 0.05
MESH = pl.DeviceIdType.MESH
HIGHEST = lax.Precision.HIGHEST
F32 = jnp.float32
BF16 = jnp.bfloat16


def term_factors():
    terms = [(4, 4, 4)] + [(a, 4, 4) for a in range(4)] + [(a, a, 4) for a in range(4)]
    terms += [(i, j, 4) for i in range(4) for j in range(i + 1, 4)]
    terms += [(a, a, a) for a in range(4)]
    terms += [(i, i, j) for i in range(4) for j in range(4) if i != j]
    terms += [(0, 1, 2), (0, 1, 3), (0, 2, 3)]
    chosen = np.zeros((3, 40, 8), np.float32)
    for k, factors in enumerate(terms):
        for place, level in enumerate(factors):
            chosen[place, k, level] = 1.0
    return chosen.reshape(120, 8)


def iota(shape, dim):
    return lax.broadcasted_iota(jnp.int32, shape, dim)


def dot_nt(a, b, precision=None):
    return lax.dot_general(
        a, b, (((1,), (1,)), ((), ())), precision=precision, preferred_element_type=F32
    )


def dot_nn(a, b, precision=None):
    return jnp.dot(a, b, precision=precision, preferred_element_type=F32)


def two_parts(x):
    first = x.astype(BF16)
    return first, (x - first.astype(F32)).astype(BF16)


def kernel(n, scen_hbm, sel_hbm, mask_hbm, y_ref, out_ref,
           scen_ref, sel_ref, mask_ref,
           ybuf, sbuf, part, r1, r2, r3, chip, pack_up, pack_low, halo, mwin, mhalo,
           lvl, mom_a, mom_b, lhs_ref,
           ins, ysem, s1s, s1r, s2s, s2r, s3s, s3r, cs, cr, hs, hr, ms, mr, ls, lr, pas, par, pbs, pbr):
    nz = n // 4
    me = lax.axis_index("cell")
    core = me % 2
    mine_y = (me // 2) % 2
    mine_z = me // 4
    chip_id = me // 2
    chips = n // 2
    sibling = me + 1 - 2 * core
    across = me + 2 - 4 * mine_y
    scens, years = y_ref.shape[0], y_ref.shape[1]
    total = scens * n

    def zone(i):
        return (mine_z + nz // 2 + i) % nz if i < nz // 2 else (mine_z + 1 + i - nz // 2) % nz if i < nz - 1 else mine_z

    def load(i):
        rows = pl.ds(pl.multiple_of(zone(i) * 16, 16), 16)
        return pltpu.make_async_copy(y_ref.at[:, :, rows, :], ybuf.at[i], ysem.at[i])

    small = [
        pltpu.make_async_copy(scen_hbm, scen_ref, ins.at[0]),
        pltpu.make_async_copy(sel_hbm, sel_ref, ins.at[1]),
        pltpu.make_async_copy(mask_hbm, mask_ref, ins.at[2]),
    ]
    for move in small:
        move.start()
    for i in range(nz):
        load(i).start()

    barrier = pltpu.get_barrier_semaphore()

    def greet(o, carry):
        pl.semaphore_signal(barrier, inc=1, device_id={"cell": lax.rem(me + o, n)}, device_id_type=MESH)
        return carry

    lax.fori_loop(1, n, greet, 0)

    for move in small:
        move.wait()
    turned = jnp.concatenate([scen_ref[...], jnp.zeros((4, 128 - scens), F32)], axis=1)
    lvl[me] = turned
    filled = ((iota((4, 128), 0) == 0) & (iota((4, 128), 1) < scens)).astype(F32)
    own = jnp.concatenate([turned, filled], axis=0)

    def copy(src, dst, send, recv, to):
        return pltpu.make_async_remote_copy(
            src_ref=src, dst_ref=dst, send_sem=send, recv_sem=recv,
            device_id={"cell": to}, device_id_type=MESH,
        )

    mask_down = copy(mask_ref, mhalo.at[0], ms.at[0], mr.at[0], (me + 1) % n)
    mask_up = copy(mask_ref, mhalo.at[1], ms.at[1], mr.at[1], (me + n - 1) % n)

    def spread(buf, send, recv):
        for o in range(1, n):
            copy(buf.at[me], buf.at[me], send, recv, lax.rem(me + o, n)).start()

    def all_but_one(buf, send, recv):
        others = buf.at[pl.ds(0, n - 1)]
        return copy(others, others, send, recv, sibling)

    def design_of(levels):
        factors = dot_nn(sel_ref[...], levels, HIGHEST)
        return factors[0:40] * factors[40:80] * factors[80:120]

    widen = (iota((KROWS, 40), 0) // 8 == iota((KROWS, 40), 1)).astype(BF16)
    low = design_of(own).astype(BF16)
    tall = dot_nn(widen, low).astype(BF16)
    by_scen = (iota((scens * 8, 128), 0) // 8 == iota((scens * 8, 128), 1)).astype(BF16)
    full = dot_nt(tall, by_scen)
    same_row = iota((KROWS, scens * 8), 0) % 8 == iota((KROWS, scens * 8), 1) % 8
    lhs_ref[...] = jnp.where(same_row, full, 0.0).astype(BF16)

    def stage1(i):
        return copy(part.at[i, 1 - core], r1.at[i], s1s.at[i], s1r.at[i], sibling)

    def stage2(i):
        return copy(part.at[i, core, 1 - mine_y], r2.at[i], s2s.at[i], s2r.at[i], across)

    def stage3(i):
        to = zone(i) * 4 + me % 4
        return copy(part.at[i, core, mine_y], r3.at[mine_z], s3s.at[i], s3r.at[mine_z], to)

    def compute(i):
        load(i).wait()

        def years_of(s, carry):
            added = jnp.sum(ybuf[i, s].astype(F32), axis=0)
            rows = pl.ds(pl.multiple_of(s * 8, 8), 8)
            sbuf[rows, 0:128] = added[0:8]
            sbuf[rows, 128:256] = added[8:16]
            return carry

        lax.fori_loop(0, scens, years_of, 0, unroll=4)
        lhs = lhs_ref[...]
        first, second = two_parts(sbuf[...])
        prod = dot_nn(lhs, first) + dot_nn(lhs, second)
        for h in range(2):
            for y in range(2):
                part[i, h, y] = prod[h * HROWS:(h + 1) * HROWS, y * 128:(y + 1) * 128]
        if i == 0:
            pl.semaphore_wait(barrier, n - 1)
        stage1(i).start()
        if i == 0:
            spread(lvl, ls, lr)
            mask_down.start()
            mask_up.start()

    def finish1(i):
        stage1(i).wait_recv()
        part[i, core, 1 - mine_y] = part[i, core, 1 - mine_y] + r1[i, 1 - mine_y]
        stage2(i).start()

    def finish2(i):
        stage2(i).wait_recv()
        added = part[i, core, mine_y] + r1[i, mine_y] + r2[i]
        if i < nz - 1:
            part[i, core, mine_y] = added
            stage3(i).start()
        else:
            r3[mine_z] = added

    for i in range(nz):
        compute(i)
        if i >= 1:
            finish1(i - 1)
        if i >= 2:
            finish2(i - 2)
    if nz >= 2:
        finish2(nz - 2)
    finish1(nz - 1)

    all_but_one(lvl, ls, lr).wait_recv()
    levels = jnp.concatenate([lvl[i] for i in range(n)], axis=1)
    levels = jnp.concatenate([levels, jnp.concatenate([filled] * n, axis=1)], axis=0)
    design = design_of(levels)
    gram = dot_nt(design, design, HIGHEST) * (1.0 / total)
    diag_block = iota((KROWS, KROWS), 0) % 8 == iota((KROWS, KROWS), 1) % 8
    gram_parts = []
    for piece in two_parts(gram):
        wide = dot_nt(dot_nn(widen, piece).astype(BF16), widen)
        gram_parts.append(jnp.where(diag_block, wide, 0.0).astype(BF16))
    g1, g2 = gram_parts

    mask_down_in = copy(mhalo.at[0], mhalo.at[0], ms.at[0], mr.at[0], (me + n - 1) % n)
    mask_up_in = copy(mhalo.at[1], mhalo.at[1], ms.at[1], mr.at[1], (me + 1) % n)
    mask_down_in.wait_recv()
    mask_up_in.wait_recv()
    mwin[0:4, :] = jnp.where(me > 0, mhalo[0].astype(F32), -1.0)
    mwin[4:8, :] = mask_ref[...].astype(F32)
    mwin[8:12, :] = jnp.where(me < n - 1, mhalo[1].astype(F32), -1.0)
    mwin[12:16, :] = jnp.full((4, 128), -1.0, F32)
    center_a, center_b = mwin[0:8, :], mwin[8:16, :]
    sub = iota((8, 128), 0)

    def north_south(a, b):
        axis = a.ndim - 2
        here = sub if a.ndim == 2 else sub[None]
        down_a, down_b = pltpu.roll(a, 1, axis), pltpu.roll(b, 1, axis)
        up_a, up_b = pltpu.roll(a, 7, axis), pltpu.roll(b, 7, axis)
        return (down_a, jnp.where(here == 0, down_a, down_b),
                jnp.where(here == 7, up_b, up_a), up_b)

    def sides(a):
        axis = a.ndim - 1
        return pltpu.roll(a, 127, axis), pltpu.roll(a, 1, axis)

    north_a, north_b, south_a, south_b = north_south(center_a, center_b)

    def weights_of(center, north, south):
        def link(near):
            return jnp.where(near >= 0.0, 0.25 + 0.75 * center * near, 0.0) * LAMBDA

        east, west = sides(center)
        links = [link(north), link(south), link(east), link(west)]
        return links + [links[0] + links[1] + links[2] + links[3] + RIDGE, center]

    weights_a = weights_of(center_a, north_a, south_a)
    weights_b = weights_of(center_b, north_b, south_b)

    finish2(nz - 1)
    for j in range(1, nz):
        source = (mine_z + j) % nz
        copy(r3.at[source], r3.at[source], s3s.at[0], s3r.at[source], source * 4 + me % 4).wait_recv()
    summed = r3[0]
    for z in range(1, nz):
        summed = summed + r3[z]
    summed = summed * (1.0 / (total * years))
    tiles = summed.reshape(HALF, 8, 128)
    front = tiles[0:PACKED]
    back = jnp.concatenate([tiles[PACKED:HALF], tiles[PACKED - 1:PACKED]], axis=0)
    upper = sub[None] < 4
    pack_up[...] = jnp.where(upper, pltpu.roll(front, 4, 1), back).reshape(PACKED * 8, 128)
    pack_low[...] = jnp.where(upper, front, pltpu.roll(back, 4, 1)).reshape(PACKED * 8, 128)
    send_up = copy(pack_up, halo.at[core], hs.at[0], hr.at[core], ((chip_id + 1) % chips) * 2)
    send_low = copy(pack_low, halo.at[core], hs.at[1], hr.at[core], ((chip_id + chips - 1) % chips) * 2 + 1)
    send_up.start()
    send_low.start()
    chip[core] = summed
    swap = copy(chip.at[core], chip.at[core], cs, cr.at[core], sibling)
    swap.start()
    copy(chip.at[1 - core], chip.at[1 - core], cs, cr.at[1 - core], sibling).wait_recv()
    near_chip = jnp.where(core == 0, (chip_id + chips - 1) % chips, (chip_id + 1) % chips)
    for h in range(2):
        copy(halo.at[h], halo.at[h], hs.at[0], hr.at[h], near_chip * 2 + h).wait_recv()
    inside = jnp.where(core == 0, chip_id > 0, chip_id < chips - 1)
    edge = []
    for h in range(2):
        got = halo[h].reshape(PACKED, 8, 128)
        edge += [got, pltpu.roll(got[0:HALF - PACKED], 4, 1)]
    edge = jnp.concatenate(edge, axis=0)
    edge = jnp.where(inside, edge, 0.0)
    whole = jnp.concatenate([chip[0], chip[1]], axis=0).reshape(TERMS, 8, 128)
    moved = pltpu.roll(whole, 4, 1)
    first = core == 0
    v0a = jnp.where(first, jnp.where(upper, edge, moved), whole)
    v0b = jnp.where(first, moved, edge)

    def gram_times(field):
        f1, f2 = two_parts(field)
        return dot_nn(g1, f1) + (dot_nn(g2, f1) + dot_nn(g1, f2))

    def image_of(tile, north, south, data, weights):
        w_n, w_s, w_e, w_w, w_all, crop = [w[None] for w in weights]
        east, west = sides(tile)
        out = w_all * tile - w_n * north - w_s * south - w_e * east - w_w * west
        return out + crop * data

    def operator(a, b, both):
        n_a, n_b, s_a, s_b = north_south(a, b)
        flat = a.reshape(KROWS, 128)
        if both:
            flat = jnp.concatenate([flat, b.reshape(KROWS, 128)], axis=1)
        data = gram_times(flat)
        out_a = image_of(a, n_a, s_a, data[:, 0:128].reshape(TERMS, 8, 128), weights_a)
        if not both:
            return out_a, None
        return out_a, image_of(b, n_b, s_b, data[:, 128:256].reshape(TERMS, 8, 128), weights_b)

    def pack(pairs):
        packed = jnp.zeros((8, 128), F32)
        for j, (p, q) in enumerate(pairs):
            tile = jnp.sum(p * q, axis=0)
            row = jnp.sum(jnp.where(sub >= 4, tile, 0.0), axis=0, keepdims=True)
            packed = jnp.where(sub == j, row, packed)
        packed = jnp.sum(packed, axis=1, keepdims=True)
        return jnp.sum(jnp.where(sub == iota((8, 128), 1), packed, 0.0), axis=0, keepdims=True)

    def sums_of(buf):
        sums = buf[0]
        for i in range(1, n):
            sums = sums + buf[i]
        sums = jnp.where(sub == iota((8, 128), 1), sums, 0.0)
        sums = jnp.broadcast_to(jnp.sum(sums, axis=1, keepdims=True), (8, 128))
        return [sums[j:j + 1, :] for j in range(7)]

    v1a, v1b = operator(v0a, v0b, True)
    mom_a[me] = pack([(v0a, v0a), (v0a, v1a), (v1a, v1a)])
    spread(mom_a, pas, par)
    v2a, v2b = operator(v1a, v1b, True)
    all_but_one(mom_a, pas, par).wait_recv()
    m = sums_of(mom_a)
    alpha0 = m[0] / m[1]
    beta0 = (m[0] - 2.0 * alpha0 * m[1] + alpha0 * alpha0 * m[2]) / m[0]
    res1 = v0a - alpha0 * v1a
    dir1 = res1 + beta0 * v0a
    image_res1 = v1a - alpha0 * v2a
    image1a = image_res1 + beta0 * v1a
    image1b = (v1b - alpha0 * v2b) + beta0 * v1b
    twice, _ = operator(image1a, image1b, False)

    mom_b[me] = pack([(res1, res1), (dir1, image1a), (res1, image1a), (image1a, image1a),
                      (res1, image_res1), (image1a, image_res1), (image1a, twice)])
    spread(mom_b, pbs, pbr)
    all_but_one(mom_b, pbs, pbr).wait_recv()
    rr, da, ra, aa, rt, at, aw = sums_of(mom_b)
    alpha1 = rr / da
    fresh = rr - 2.0 * alpha1 * ra + alpha1 * alpha1 * aa
    beta1 = fresh / rr
    along = (rt + 2.0 * beta1 * ra - 2.0 * alpha1 * at - 2.0 * alpha1 * beta1 * aa
             + alpha1 * alpha1 * aw + beta1 * beta1 * da)
    alpha2 = fresh / along
    res2 = res1 - alpha1 * image1a
    dir2 = res2 + beta1 * dir1
    image2 = image_res1 - alpha1 * twice + beta1 * image1a
    solved = alpha0 * v0a + alpha1 * dir1 + alpha2 * dir2
    out_ref[...] = jnp.where(upper, pltpu.roll(solved, 4, 1), res2 - alpha2 * image2)

    all_but_one(lvl, ls, lr).wait_send()
    all_but_one(mom_a, pas, par).wait_send()
    all_but_one(mom_b, pbs, pbr).wait_send()
    mask_down.wait_send()
    mask_up.wait_send()
    for i in range(nz):
        stage1(i).wait_send()
        stage2(i).wait_send()
        if i < nz - 1:
            stage3(i).wait_send()
    swap.wait_send()
    send_up.wait_send()
    send_low.wait_send()


def body(n, scen_inputs, yields, crop_mask):
    nz = n // 4
    scens, years = yields.shape[0], yields.shape[1]
    vmem = pl.BlockSpec(memory_space=pltpu.VMEM)
    hbm = pl.BlockSpec(memory_space=pltpu.HBM)
    dma = pltpu.SemaphoreType.DMA
    both = pl.pallas_call(
        functools.partial(kernel, n),
        out_shape=jax.ShapeDtypeStruct((TERMS, 8, 128), F32),
        in_specs=[hbm, hbm, hbm, hbm],
        out_specs=vmem,
        scratch_shapes=[
            pltpu.VMEM((4, scens), F32),
            pltpu.VMEM((120, 8), F32),
            pltpu.VMEM((4, 128), jnp.int32),
            pltpu.VMEM((nz, scens, years, 16, 128), BF16),
            pltpu.VMEM((scens * 8, 256), F32),
            pltpu.VMEM((nz, 2, 2, HROWS, 128), F32),
            pltpu.VMEM((nz, 2, HROWS, 128), F32),
            pltpu.VMEM((nz, HROWS, 128), F32),
            pltpu.VMEM((nz, HROWS, 128), F32),
            pltpu.VMEM((2, HROWS, 128), F32),
            pltpu.VMEM((PACKED * 8, 128), F32),
            pltpu.VMEM((PACKED * 8, 128), F32),
            pltpu.VMEM((2, PACKED * 8, 128), F32),
            pltpu.VMEM((16, 128), F32),
            pltpu.VMEM((2, 4, 128), jnp.int32),
            pltpu.VMEM((n, 4, 128), F32),
            pltpu.VMEM((n, 1, 128), F32),
            pltpu.VMEM((n, 1, 128), F32),
            pltpu.VMEM((KROWS, scens * 8), BF16),
            dma((3,)), dma((nz,)),
            dma((nz,)), dma((nz,)),
            dma((nz,)), dma((nz,)),
            dma((nz,)), dma((nz,)),
            dma, dma((2,)),
            dma((2,)), dma((2,)),
            dma((2,)), dma((2,)),
            dma, dma, dma, dma, dma, dma,
        ],
        compiler_params=pltpu.CompilerParams(
            collective_id=0, has_side_effects=True, vmem_limit_bytes=64512 * 1024
        ),
    )(scen_inputs.T, jnp.asarray(term_factors()), crop_mask, yields)
    both = jnp.transpose(both, (1, 0, 2))
    return both[0:4], both[4:8]


def solution(mesh):
    in_specs = (P("cell", None), P("cell", None, None, "group"), P("cell", "group"))
    out_specs = (P("cell", None, "group"), P("cell", None, "group"))
    return jax.shard_map(
        functools.partial(body, mesh.shape["cell"]),
        mesh=mesh, in_specs=in_specs, out_specs=out_specs, check_vma=False,
    )
```
